32 devices in a mesh: groups: 2 (over y), query: 16 (over z, x, core).
Axes of the slice: x: 2, y: 2, z: 4, core: 2. Of those that a mesh axis runs over, the one named last changes fastest.
Arguments:
- tokens: bfloat16 [32, 8192], P(('groups', 'query')), parts along dimension 0, may hold values from -6 to 6
- target: bfloat16 [32, 8192], P(('groups', 'query')), parts along dimension 0, may hold values from -6 to 6
- gate_weight: bfloat16 [8192, 28672], P(None, 'query'), may hold values from -0.0625 to 0.0625
- up_weight: bfloat16 [8192, 28672], P(None, 'query'), may hold values from -0.0625 to 0.0625
- down_weight: bfloat16 [28672, 8192], P('query'), may hold values from -0.03125 to 0.03125
- proj_in: bfloat16 [28672, 64], P('query'), may hold values from -0.03125 to 0.03125
- proj_out: bfloat16 [8192, 64], replicated, may hold values from -0.0625 to 0.0625
- segment_ids: int32 [32], P('groups'), parts along dimension 0, may hold values from 0 to 3, never falling along the last dimension, each value on 1 to 8 neighbouring positions
- queries: bfloat16 [1024, 4096], P('query'), may hold values from -0.09375 to 0.09375
Outputs:
- scores: float32 [1024, 8], P('query', 'groups'), parts along dimension 1
The draws below stay inside these ranges and needn't reach their ends.
There are 2 independent parts, one for each index of `groups`. The reference program is written for one: setup_inputs(seed, part) draws one part's arguments, and reference() takes and returns one part's arrays. A program takes and returns all parts, laid end to end along the dimension named above; an argument that names none is the same for every part. Nothing has to cross between parts.
Inputs may be any that keep to these rules, and one draw needn't show every extreme that they name: `segment_ids`: ids never fall along the batch; each of the 4 pieces holds 1 to 8 tokens and one holds exactly 8.
All inputs are finite; a program needn't handle non-finite values.
Results may differ from the reference program's by a relative error of at most 0.0049.
Values may be sent and summed in bfloat16 or wider, within the bound.
A program may use at most 192 MiB of HBM per device.

```python
import math
import jax
import jax.numpy as jnp
import numpy as np
from jax import lax

D = 8192
FF = 28672
R = 64
SEQS = 4
TOKENS = 16
NQ = 1024
MOST = 8


def levels(key, extent, pieces, least, high):
    factor_of, own = 1.0, jax.random.fold_in(key, 6)
    for position, blocks in pieces:
        draws = jnp.exp(jax.random.uniform(jax.random.fold_in(own, position), (blocks,), jnp.float32, least / len(pieces), high / len(pieces)))
        factor_of = factor_of * jnp.repeat(draws, extent[position] // blocks).reshape([-1 if axis == position else 1 for axis in range(len(extent))])
    return factor_of


def length_profile(number_of, total, reach, skew):
    loads = [(1 << 20) // math.isqrt(grade ** skew) + 1 for grade in range(2, number_of + 1)]
    surplus, counts = total - reach - (number_of - 1), [1] * (number_of - 1)
    while surplus > 0:
        free = [i for i in range(number_of - 1) if counts[i] < reach]
        whole, left = sum([loads[i] for i in free]), surplus
        for i in free:
            extra = min(reach - counts[i], max(1, left * loads[i] // whole), surplus)
            counts[i] = counts[i] + extra
            surplus = surplus - extra
    return np.array([reach] + counts)


def uneven_parts(own_key, number_of, total, limit, skew):
    if number_of == 2:
        one = jax.random.randint(own_key, (), max(1, total - limit), min(limit, total - 1) + 1)
        return jnp.stack([one, total - one])
    lengths = jnp.asarray(length_profile(number_of, total, limit, skew), jnp.int32)
    pairs = (number_of - 1) // 2
    donor, sink = lengths[1:1 + 2 * pairs:2], lengths[2:2 + 2 * pairs:2]
    room = jnp.minimum(donor - 1, limit - sink)
    moved = jax.random.randint(jax.random.fold_in(own_key, 1), (pairs,), 0, 1 << 20) % (room + 1)
    lengths = lengths.at[1:1 + 2 * pairs:2].set(donor - moved).at[2:2 + 2 * pairs:2].set(sink + moved)
    return lengths[jax.random.permutation(jax.random.fold_in(own_key, 2), number_of)]


def normal_values(own_key, dims, width, limit, pieces=(), kind=jnp.bfloat16):
    factor_of = levels(own_key, dims, pieces, -0.22, 0.18) if pieces else 1.0
    values = jax.random.normal(own_key, dims, jnp.float32) * width * factor_of
    return jnp.minimum(jnp.maximum(values, -limit), limit).astype(kind)


def setup_inputs(seed: int = 0, part: int = 0) -> dict:
    keys = jax.random.split(jax.random.key(seed), 10)
    own_keys = jax.random.split(jax.random.fold_in(keys[9], part), 10)
    return {
        "tokens": normal_values(own_keys[0], (TOKENS, D), 1.0, 6.0, ((0, 16),)),
        "target": normal_values(own_keys[1], (TOKENS, D), 1.0, 6.0, ((0, 16),)),
        "gate_weight": normal_values(keys[2], (D, FF), D ** -0.5, 0.0625, ((1, 16),)),
        "up_weight": normal_values(keys[3], (D, FF), D ** -0.5, 0.0625, ((1, 16),)),
        "down_weight": normal_values(keys[4], (FF, D), FF ** -0.5, 0.03125, ((0, 16),)),
        "proj_in": normal_values(keys[5], (FF, R), FF ** -0.5, 0.03125, ((0, 16),)),
        "proj_out": normal_values(keys[6], (D, R), D ** -0.5, 0.0625),
        "segment_ids": jnp.searchsorted(jnp.cumsum(uneven_parts(own_keys[7], SEQS, TOKENS, MOST, 1)), jnp.arange(TOKENS), side="right").astype(jnp.int32),
        "queries": normal_values(keys[8], (NQ, R * R), (R * R) ** -0.5, 0.09375, ((0, 16),)),
    }


def reference(tokens, target, gate_weight, up_weight, down_weight, proj_in, proj_out, segment_ids, queries):
    gate_pre = jnp.dot(tokens, gate_weight, preferred_element_type=jnp.float32)
    up_pre = jnp.dot(tokens, up_weight, preferred_element_type=jnp.float32)
    hidden = (jax.nn.silu(gate_pre) * up_pre).astype(jnp.bfloat16)
    output = jnp.dot(hidden, down_weight, preferred_element_type=jnp.float32)
    grad = output - target.astype(jnp.float32)
    input_side = jnp.dot(hidden, proj_in, preferred_element_type=jnp.float32)
    output_side = jnp.dot(grad, proj_out.astype(jnp.float32), precision=lax.Precision.HIGHEST)
    seq_index = jnp.arange(SEQS, dtype=jnp.int32)
    onehot = (segment_ids[None, :] == seq_index[:, None]).astype(jnp.float32)
    masked = onehot[:, :, None] * input_side[None, :, :]
    kronecker = jnp.einsum("sti,tj->sij", masked, output_side, precision=lax.Precision.HIGHEST)
    kronecker = kronecker.reshape(SEQS, R * R).astype(jnp.bfloat16)
    return jnp.dot(queries, kronecker.T, preferred_element_type=jnp.float32)
```

```python
import functools

import jax
import jax.numpy as jnp
from jax import lax
from jax.experimental import pallas as pl
from jax.experimental.pallas import tpu as pltpu
from jax.sharding import PartitionSpec as P

SEQS = 4
DEPTH = 512
SLOTS = 5
F32 = jnp.float32
BF16 = jnp.bfloat16
MESH = pl.DeviceIdType.MESH


def rows_per_chunk(total, most):
    return max(size for size in range(16, most + 1, 16) if total % size == 0)


def split(value):
    high = value.astype(BF16)
    return high, (value - high.astype(F32)).astype(BF16)


def kernel(
    n, tokens, target, gate, up, down, proj_in, proj_out, segment_ids, queries, scores,
    gate_ring, up_ring, down_buf, pin, pout, tgt, qbuf, gathered, x32, x16, expand, mixed,
    gate_acc, up_acc, payload, parts,
    gate_sem, up_sem, down_sem, load_sem, tok_send, tok_recv, part_send, part_recv,
):
    me = lax.axis_index("query")
    width, hidden_units = gate.shape
    rank = proj_in.shape[1]
    count = x16.shape[0]
    down_rows = down_buf.shape[1]
    down_chunks = down_buf.shape[0]
    steps = width // DEPTH
    slots = gate_ring.shape[0]

    def peer(d):
        return lax.rem(me + d, n)

    barrier = pltpu.get_barrier_semaphore()

    @pl.loop(1, n)
    def _(d):
        pl.semaphore_signal(barrier, inc=1, device_id={"query": peer(d)}, device_id_type=MESH)

    loads = [
        pltpu.make_async_copy(src, dst, load_sem.at[i])
        for i, (src, dst) in enumerate(
            [
                (proj_out, pout),
                (tokens, gathered.at[me]),
                (target, tgt),
                (proj_in, pin),
                (queries, qbuf),
            ]
        )
    ]

    def down_copy(c):
        at = pl.ds(pl.multiple_of(c * down_rows, down_rows), down_rows)
        return pltpu.make_async_copy(down.at[at, :], down_buf.at[c], down_sem.at[c])

    def ring_copies(c, slot):
        at = pl.ds(pl.multiple_of(c * DEPTH, DEPTH), DEPTH)
        return (
            pltpu.make_async_copy(gate.at[at, :], gate_ring.at[slot], gate_sem.at[slot]),
            pltpu.make_async_copy(up.at[at, :], up_ring.at[slot], up_sem.at[slot]),
        )

    for load in loads[:4]:
        load.start()
    for c in range(down_chunks):
        down_copy(c).start()
    for c in range(slots):
        for copy in ring_copies(c, c):
            copy.start()

    pl.semaphore_wait(barrier, n - 1)

    def token_copy(d):
        return pltpu.make_async_remote_copy(
            src_ref=tokens,
            dst_ref=gathered.at[me],
            send_sem=tok_send.at[d],
            recv_sem=tok_recv.at[me],
            device_id={"query": peer(d)},
            device_id_type=MESH,
        )

    @pl.loop(1, n)
    def _(d):
        token_copy(d).start()

    owner = lax.broadcasted_iota(jnp.int32, expand.shape, 1) // rank
    expand[...] = jnp.where(
        lax.broadcasted_iota(jnp.int32, expand.shape, 0) == owner, 1.0, 0.0
    ).astype(BF16)
    gate_acc[...] = jnp.zeros_like(gate_acc)
    up_acc[...] = jnp.zeros_like(up_acc)

    for load in loads[:4]:
        load.wait()
    target_side = jnp.dot(tgt[...], pout[...], preferred_element_type=F32)

    @pl.loop(0, down_chunks)
    def _(c):
        down_copy(c).wait()
        side = jnp.dot(down_buf[c], pout[...], preferred_element_type=F32)
        at = pl.ds(pl.multiple_of(c * down_rows, down_rows), down_rows)
        high, low = split(jnp.concatenate([pin[at, :].astype(F32), side], axis=1))
        mixed[at, : 2 * rank] = high
        mixed[at, 2 * rank :] = low

    @pl.loop(1, n)
    def _(d):
        source = peer(d)
        pltpu.make_async_remote_copy(
            src_ref=tokens,
            dst_ref=gathered.at[source],
            send_sem=tok_send.at[d],
            recv_sem=tok_recv.at[source],
            device_id={"query": source},
            device_id_type=MESH,
        ).wait_recv()

    @pl.loop(0, n)
    def _(t):
        x32[pl.ds(t, 1), :] = gathered[t].astype(F32)

    x16[...] = x32[...].astype(BF16)
    loads[4].start()

    @pl.loop(0, steps)
    def _(c):
        slot = lax.rem(c, slots)
        for copy in ring_copies(c, slot):
            copy.wait()
        x = x16[:, pl.ds(pl.multiple_of(c * DEPTH, DEPTH), DEPTH)]
        gate_acc[...] += jnp.dot(x, gate_ring[slot], preferred_element_type=F32)
        up_acc[...] += jnp.dot(x, up_ring[slot], preferred_element_type=F32)

        @pl.when(c + slots < steps)
        def _():
            for copy in ring_copies(c + slots, slot):
                copy.start()

    gate_pre = gate_acc[...]
    hidden = (gate_pre / (1.0 + jnp.exp(-gate_pre)) * up_acc[...]).astype(BF16)
    sides = jnp.dot(hidden, mixed[...], preferred_element_type=F32)
    sides = sides[:, : 2 * rank] + sides[:, 2 * rank :]
    shifted = jnp.concatenate([jnp.zeros_like(target_side), target_side], axis=1)
    own_row = lax.broadcasted_iota(jnp.int32, sides.shape, 0) == me
    sides = sides - jnp.where(own_row, jnp.broadcast_to(shifted, sides.shape), 0.0)
    payload[...] = sides.astype(payload.dtype)

    def part_copy(d, slot):
        return pltpu.make_async_remote_copy(
            src_ref=payload,
            dst_ref=parts.at[slot],
            send_sem=part_send.at[d],
            recv_sem=part_recv.at[slot],
            device_id={"query": peer(d)},
            device_id_type=MESH,
        )

    @pl.loop(1, n)
    def _(d):
        part_copy(d, me).start()

    parts[me] = payload[...]
    loads[4].wait()
    marks = (
        lax.broadcasted_iota(jnp.int32, (2 * SEQS, count), 0) == segment_ids[...]
    ).astype(BF16)

    @pl.loop(1, n)
    def _(d):
        part_copy(d, peer(d)).wait_recv()

    total = lax.fori_loop(
        0, n, lambda p, t: t + parts[p].astype(F32), jnp.zeros(payload.shape, F32)
    )
    high, low = split(total)
    spread = jnp.dot(
        jnp.concatenate([high, low], axis=0), expand[...], preferred_element_type=F32
    )
    spread = spread[:count] + spread[count:]
    output_side = total[:, rank:]
    doubled = jnp.concatenate([output_side, output_side], axis=1)
    pairs = spread * jnp.concatenate([doubled] * (rank // 2), axis=1)
    high, low = split(pairs)
    kronecker = jnp.dot(marks, high, preferred_element_type=F32) + jnp.dot(
        marks, low, preferred_element_type=F32
    )
    result = lax.dot_general(
        qbuf[...],
        kronecker.astype(BF16),
        (((1,), (1,)), ((), ())),
        preferred_element_type=F32,
    )
    scores[...] = result[:, :SEQS]

    @pl.loop(1, n)
    def _(d):
        token_copy(d).wait_send()
        part_copy(d, me).wait_send()


def solution(mesh):
    n = mesh.shape["query"]

    def local(tokens, target, gate, up, down, proj_in, proj_out, segment_ids, queries):
        width, units = gate.shape
        rank = proj_in.shape[1]
        count = segment_ids.shape[0]
        down_rows = rows_per_chunk(units, 256)
        down_chunks = units // down_rows
        any_spec = pl.BlockSpec(memory_space=pl.ANY)
        vmem_spec = pl.BlockSpec(memory_space=pltpu.VMEM)
        dma = pltpu.SemaphoreType.DMA
        return pl.pallas_call(
            functools.partial(kernel, n),
            out_shape=jax.ShapeDtypeStruct((queries.shape[0], SEQS), F32),
            in_specs=[any_spec] * 7 + [vmem_spec, any_spec],
            out_specs=vmem_spec,
            scratch_shapes=[
                pltpu.VMEM((SLOTS, DEPTH, units), BF16),
                pltpu.VMEM((SLOTS, DEPTH, units), BF16),
                pltpu.VMEM((down_chunks, down_rows, width), BF16),
                pltpu.VMEM((units, rank), BF16),
                pltpu.VMEM((width, rank), BF16),
                pltpu.VMEM((1, width), BF16),
                pltpu.VMEM(queries.shape, BF16),
                pltpu.VMEM((n, 1, width), BF16),
                pltpu.VMEM((count, width), F32),
                pltpu.VMEM((count, width), BF16),
                pltpu.VMEM((2 * rank, rank * rank), BF16),
                pltpu.VMEM((units, 4 * rank), BF16),
                pltpu.VMEM((count, units), F32),
                pltpu.VMEM((count, units), F32),
                pltpu.VMEM((count, 2 * rank), F32),
                pltpu.VMEM((n, count, 2 * rank), F32),
                dma((SLOTS,)),
                dma((SLOTS,)),
                dma((down_chunks,)),
                dma((5,)),
                dma((n,)),
                dma((n,)),
                dma((n,)),
                dma((n,)),
            ],
            compiler_params=pltpu.CompilerParams(
                collective_id=0, has_side_effects=True, vmem_limit_bytes=63 * 1024 * 1024
            ),
            name="forget",
        )(
            tokens, target, gate, up, down, proj_in, proj_out,
            segment_ids.reshape(1, count), queries,
        )

    in_specs = (
        P(("groups", "query"), None),
        P(("groups", "query"), None),
        P(None, "query"),
        P(None, "query"),
        P("query", None),
        P("query", None),
        P(),
        P("groups"),
        P("query", None),
    )
    return jax.shard_map(
        local, mesh=mesh, in_specs=in_specs, out_specs=P("query", "groups"), check_vma=False
    )
```

```python
import functools

import jax
import jax.numpy as jnp
from jax import lax
from jax.experimental import pallas as pl
from jax.experimental.pallas import tpu as pltpu
from jax.sharding import PartitionSpec as P

SEQS = 4
DEPTH = 512
SLOTS = 10
DOWN_SLOTS = 8
LANES = 128
F32 = jnp.float32
BF16 = jnp.bfloat16
MESH = pl.DeviceIdType.MESH


def split(value):
    high = value.astype(BF16)
    return high, (value - high.astype(F32)).astype(BF16)


def dot(a, b):
    return jnp.dot(a, b, preferred_element_type=F32)


def dot_lanes(a, b):
    return lax.dot_general(a, b, (((1,), (1,)), ((), ())), preferred_element_type=F32)


def pack(value):
    half = value.shape[0] // 2
    return jnp.concatenate([value[:half], value[half:]], axis=1)


def kernel(
    n, tokens, target, gate, up, down, proj_in, proj_out, segment_ids, queries, scores,
    gate_ring, up_ring, down_ring, pin, pout, tok, tgt, qbuf, slab32, slab, gathered, x32, x16,
    expand, spread, gate_acc, up_acc, hidden_ref, side_acc, payload_a, payload_b, parts_a, parts_b,
    gate_sem, up_sem, down_sem, load_sem, tok_send, tok_recv, a_send, a_recv, b_send, b_recv,
):
    me = lax.axis_index("query")
    width = gate.shape[0]
    rank = proj_in.shape[0]
    count = x16.shape[0]
    pieces = width // LANES
    steps = width // DEPTH
    slots = gate_ring.shape[0]
    down_slots = down_ring.shape[0]

    def peer(d):
        return lax.rem(me + d, n)

    barrier = pltpu.get_barrier_semaphore()

    @pl.loop(1, n)
    def _(d):
        pl.semaphore_signal(barrier, inc=1, device_id={"query": peer(d)}, device_id_type=MESH)

    loads = [
        pltpu.make_async_copy(src, dst, load_sem.at[i])
        for i, (src, dst) in enumerate(
            [(tokens, tok), (target, tgt), (proj_out, pout), (proj_in, pin), (queries, qbuf)]
        )
    ]

    def chunk(c):
        return pl.ds(pl.multiple_of(c * DEPTH, DEPTH), DEPTH)

    def ring_copies(c, slot):
        return (
            pltpu.make_async_copy(gate.at[chunk(c), :], gate_ring.at[slot], gate_sem.at[slot]),
            pltpu.make_async_copy(up.at[chunk(c), :], up_ring.at[slot], up_sem.at[slot]),
        )

    def down_copy(c):
        slot = lax.rem(c, down_slots)
        return pltpu.make_async_copy(down.at[:, chunk(c)], down_ring.at[slot], down_sem.at[slot])

    for load in loads[:3]:
        load.start()
    for c in range(slots):
        for copy in ring_copies(c, c):
            copy.start()
    loads[3].start()
    loads[4].start()

    loads[0].wait()
    for k in range(pieces):
        slab32[k : k + 1, :] = tok[:, k * LANES : (k + 1) * LANES].astype(F32)
    slab[...] = slab32[...].astype(BF16)
    gathered[me] = slab[...]

    pl.semaphore_wait(barrier, n - 1)

    def push(src, dst, send, recv, d, slot):
        return pltpu.make_async_remote_copy(
            src_ref=src,
            dst_ref=dst.at[slot],
            send_sem=send.at[d],
            recv_sem=recv.at[slot],
            device_id={"query": peer(d)},
            device_id_type=MESH,
        )

    token_push = functools.partial(push, slab, gathered, tok_send, tok_recv)
    a_push = functools.partial(push, payload_a, parts_a, a_send, a_recv)
    b_push = functools.partial(push, payload_b, parts_b, b_send, b_recv)

    def start_all(copy):
        @pl.loop(1, n)
        def _(d):
            copy(d, me).start()

    def receive_all(copy):
        @pl.loop(1, n)
        def _(d):
            copy(d, peer(d)).wait_recv()

    start_all(token_push)

    owner = lax.broadcasted_iota(jnp.int32, expand.shape, 1) // rank
    expand[...] = jnp.where(
        lax.broadcasted_iota(jnp.int32, expand.shape, 0) == owner, 1.0, 0.0
    ).astype(BF16)
    gate_acc[...] = jnp.zeros_like(gate_acc)
    up_acc[...] = jnp.zeros_like(up_acc)
    side_acc[...] = jnp.zeros_like(side_acc)
    loads[1].wait()
    loads[2].wait()
    target_side = dot_lanes(tgt[...], pout[...])

    receive_all(token_push)
    x32[...] = gathered[...].reshape(n * pieces, LANES).astype(F32)
    for k in range(pieces):
        x16[:, k * LANES : (k + 1) * LANES] = x32[pl.ds(k, n, stride=pieces), :].astype(BF16)

    @pl.loop(0, steps)
    def _(c):
        slot = lax.rem(c, slots)
        for copy in ring_copies(c, slot):
            copy.wait()
        x = x16[:, chunk(c)]
        gate_acc[...] += dot(x, gate_ring[slot])
        up_acc[...] += dot(x, up_ring[slot])

        @pl.when(c + slots < steps)
        def _():
            for copy in ring_copies(c + slots, slot):
                copy.start()

        @pl.when(c < down_slots)
        def _():
            down_copy(c).start()

    gate_pre = gate_acc[...]
    hidden = (gate_pre / (1.0 + jnp.exp(-gate_pre)) * up_acc[...]).astype(BF16)
    hidden_ref[...] = hidden
    loads[3].wait()
    payload_a[...] = pack(dot_lanes(hidden, pin[...]))
    start_all(a_push)
    parts_a[me] = payload_a[...]

    def down_step(c):
        down_copy(c).wait()
        high, low = split(dot(hidden_ref[...], down_ring[lax.rem(c, down_slots)]))
        side_acc[...] += dot_lanes(jnp.concatenate([high, low], axis=0), pout[:, chunk(c)])

        @pl.when(c + down_slots < steps)
        def _():
            down_copy(c + down_slots).start()

    def sum_parts(parts):
        return lax.fori_loop(
            0, n, lambda p, t: t + parts[p], jnp.zeros(parts.shape[1:], F32)
        )

    pl.loop(0, steps // 2)(down_step)

    receive_all(a_push)
    total = sum_parts(parts_a)
    input_side = jnp.concatenate([total[:, :rank], total[:, rank:]], axis=0)
    high, low = split(input_side)
    wide = dot(jnp.concatenate([high, low], axis=0), expand[...])
    spread[...] = wide[:count] + wide[count:]
    loads[4].wait()

    pl.loop(steps // 2, steps)(down_step)

    side = side_acc[:count, :] + side_acc[count:, :]
    own_row = lax.broadcasted_iota(jnp.int32, side.shape, 0) == me
    side = side - jnp.where(own_row, jnp.broadcast_to(target_side, side.shape), 0.0)
    payload_b[...] = pack(side)
    start_all(b_push)
    parts_b[me] = payload_b[...]
    marks = (
        lax.broadcasted_iota(jnp.int32, (2 * SEQS, count), 0) == segment_ids[...]
    ).astype(BF16)

    receive_all(b_push)
    total = sum_parts(parts_b)
    first, second = total[:, :rank], total[:, rank:]
    doubled = jnp.concatenate(
        [jnp.concatenate([first, first], axis=1), jnp.concatenate([second, second], axis=1)],
        axis=0,
    )
    pairs = spread[...] * jnp.concatenate([doubled] * (rank // 2), axis=1)
    high, low = split(pairs)
    kronecker = dot(marks, high) + dot(marks, low)
    scores[...] = dot_lanes(kronecker.astype(BF16), qbuf[...])[:SEQS]

    @pl.loop(1, n)
    def _(d):
        token_push(d, me).wait_send()
        a_push(d, me).wait_send()
        b_push(d, me).wait_send()


def solution(mesh):
    n = mesh.shape["query"]

    def local(tokens, target, gate, up, down, proj_in, proj_out, segment_ids, queries):
        width, units = gate.shape
        rank = proj_in.shape[1]
        count = segment_ids.shape[0]
        pieces = width // LANES
        any_spec = pl.BlockSpec(memory_space=pl.ANY)
        vmem_spec = pl.BlockSpec(memory_space=pltpu.VMEM)
        dma = pltpu.SemaphoreType.DMA
        return pl.pallas_call(
            functools.partial(kernel, n),
            out_shape=jax.ShapeDtypeStruct((SEQS, queries.shape[0]), F32),
            in_specs=[any_spec] * 7 + [vmem_spec, any_spec],
            out_specs=vmem_spec,
            scratch_shapes=[
                pltpu.VMEM((SLOTS, DEPTH, units), BF16),
                pltpu.VMEM((SLOTS, DEPTH, units), BF16),
                pltpu.VMEM((DOWN_SLOTS, units, DEPTH), BF16),
                pltpu.VMEM((rank, units), BF16),
                pltpu.VMEM((rank, width), BF16),
                pltpu.VMEM((1, width), BF16),
                pltpu.VMEM((1, width), BF16),
                pltpu.VMEM(queries.shape, BF16),
                pltpu.VMEM((pieces, LANES), F32),
                pltpu.VMEM((pieces, LANES), BF16),
                pltpu.VMEM((n, pieces, LANES), BF16),
                pltpu.VMEM((n * pieces, LANES), F32),
                pltpu.VMEM((count, width), BF16),
                pltpu.VMEM((rank, rank * rank), BF16),
                pltpu.VMEM((count, rank * rank), F32),
                pltpu.VMEM((count, units), F32),
                pltpu.VMEM((count, units), F32),
                pltpu.VMEM((count, units), BF16),
                pltpu.VMEM((2 * count, rank), F32),
                pltpu.VMEM((count // 2, 2 * rank), F32),
                pltpu.VMEM((count // 2, 2 * rank), F32),
                pltpu.VMEM((n, count // 2, 2 * rank), F32),
                pltpu.VMEM((n, count // 2, 2 * rank), F32),
                dma((SLOTS,)),
                dma((SLOTS,)),
                dma((DOWN_SLOTS,)),
                dma((5,)),
                dma((n,)),
                dma((n,)),
                dma((n,)),
                dma((n,)),
                dma((n,)),
                dma((n,)),
            ],
            compiler_params=pltpu.CompilerParams(
                collective_id=0, has_side_effects=True, vmem_limit_bytes=63 * 1024 * 1024
            ),
            name="forget",
        )(
            tokens, target, gate, up, down, proj_in.T, proj_out.T,
            segment_ids.reshape(1, count), queries,
        ).T

    in_specs = (
        P(("groups", "query"), None),
        P(("groups", "query"), None),
        P(None, "query"),
        P(None, "query"),
        P("query", None),
        P("query", None),
        P(),
        P("groups"),
        P("query", None),
    )
    return jax.shard_map(
        local, mesh=mesh, in_specs=in_specs, out_specs=P("query", "groups"), check_vma=False
    )
```

```python
import functools

import jax
import jax.numpy as jnp
from jax import lax
from jax.experimental import pallas as pl
from jax.experimental.pallas import tpu as pltpu
from jax.sharding import PartitionSpec as P

SEQS = 4
DEPTH = 1024
SLOTS = 5
DOWN_SLOTS = 4
LANES = 128
F32 = jnp.float32
BF16 = jnp.bfloat16
MESH = pl.DeviceIdType.MESH


def split(value):
    high = value.astype(BF16)
    return high, (value - high.astype(F32)).astype(BF16)


def dot(a, b):
    return jnp.dot(a, b, preferred_element_type=F32)


def dot_lanes(a, b):
    return lax.dot_general(a, b, (((1,), (1,)), ((), ())), preferred_element_type=F32)


def pack(value):
    half = value.shape[0] // 2
    return jnp.concatenate([value[:half], value[half:]], axis=1)


def kernel(
    n, tokens, target, gate, up, down, proj_in, proj_out, segment_ids, queries, scores,
    gate_ring, up_ring, down_ring, pin, pout, tok, tgt, qbuf, slab32, slab, gathered, x32, x16,
    expand, spread, gate_acc, up_acc, hidden_ref, block, side_acc, payload_a, payload_b, parts_a, parts_b,
    gate_sem, up_sem, down_sem, load_sem, tok_send, tok_recv, a_send, a_recv, b_send, b_recv,
):
    me = lax.axis_index("query")
    width = gate.shape[0]
    rank = proj_in.shape[0]
    count = x16.shape[0]
    pieces = width // LANES
    steps = width // DEPTH
    slots = gate_ring.shape[0]
    down_slots = down_ring.shape[0]

    def peer(d):
        return lax.rem(me + d, n)

    barrier = pltpu.get_barrier_semaphore()

    @pl.loop(1, n)
    def _(d):
        pl.semaphore_signal(barrier, inc=1, device_id={"query": peer(d)}, device_id_type=MESH)

    loads = [
        pltpu.make_async_copy(src, dst, load_sem.at[i])
        for i, (src, dst) in enumerate(
            [(tokens, tok), (target, tgt), (proj_out, pout), (proj_in, pin), (queries, qbuf)]
        )
    ]

    def chunk(c):
        return pl.ds(pl.multiple_of(c * DEPTH, DEPTH), DEPTH)

    def ring_copies(c, slot):
        return (
            pltpu.make_async_copy(gate.at[chunk(c), :], gate_ring.at[slot], gate_sem.at[slot]),
            pltpu.make_async_copy(up.at[chunk(c), :], up_ring.at[slot], up_sem.at[slot]),
        )

    def down_copy(c):
        slot = lax.rem(c, down_slots)
        return pltpu.make_async_copy(down.at[:, chunk(c)], down_ring.at[slot], down_sem.at[slot])

    for load in loads[:3]:
        load.start()
    for c in range(slots):
        for copy in ring_copies(c, c):
            copy.start()
    loads[3].start()
    loads[4].start()

    loads[0].wait()
    for k in range(pieces):
        slab32[k : k + 1, :] = tok[:, k * LANES : (k + 1) * LANES].astype(F32)
    slab[...] = slab32[...].astype(BF16)
    gathered[me] = slab[...]

    pl.semaphore_wait(barrier, n - 1)

    def push(src, dst, send, recv, d, slot):
        return pltpu.make_async_remote_copy(
            src_ref=src,
            dst_ref=dst.at[slot],
            send_sem=send.at[d],
            recv_sem=recv.at[slot],
            device_id={"query": peer(d)},
            device_id_type=MESH,
        )

    token_push = functools.partial(push, slab, gathered, tok_send, tok_recv)
    a_push = functools.partial(push, payload_a, parts_a, a_send, a_recv)
    b_push = functools.partial(push, payload_b, parts_b, b_send, b_recv)

    def start_all(copy):
        @pl.loop(1, n)
        def _(d):
            copy(d, me).start()

    def receive_all(copy):
        @pl.loop(1, n)
        def _(d):
            copy(d, peer(d)).wait_recv()

    start_all(token_push)

    owner = lax.broadcasted_iota(jnp.int32, expand.shape, 1) // rank
    expand[...] = jnp.where(
        lax.broadcasted_iota(jnp.int32, expand.shape, 0) == owner, 1.0, 0.0
    ).astype(BF16)
    gate_acc[...] = jnp.zeros_like(gate_acc)
    up_acc[...] = jnp.zeros_like(up_acc)
    side_acc[...] = jnp.zeros_like(side_acc)
    loads[1].wait()
    loads[2].wait()
    target_side = dot_lanes(tgt[...], pout[...])

    receive_all(token_push)
    x32[...] = gathered[...].reshape(n * pieces, LANES).astype(F32)
    for k in range(pieces):
        x16[:, k * LANES : (k + 1) * LANES] = x32[pl.ds(k, n, stride=pieces), :].astype(BF16)

    @pl.loop(0, steps)
    def _(c):
        slot = lax.rem(c, slots)
        for copy in ring_copies(c, slot):
            copy.wait()
        x = x16[:, chunk(c)]
        gate_acc[...] += dot(x, gate_ring[slot])
        up_acc[...] += dot(x, up_ring[slot])

        @pl.when(c + slots < steps)
        def _():
            for copy in ring_copies(c + slots, slot):
                copy.start()

        @pl.when(c < down_slots)
        def _():
            down_copy(c).start()

    gate_pre = gate_acc[...]
    hidden = (gate_pre / (1.0 + jnp.exp(-gate_pre)) * up_acc[...]).astype(BF16)
    hidden_ref[...] = hidden
    loads[3].wait()
    payload_a[...] = pack(dot_lanes(hidden, pin[...]))
    start_all(a_push)
    parts_a[me] = payload_a[...]

    def down_dot(c):
        down_copy(c).wait()
        high, low = split(dot(hidden_ref[...], down_ring[lax.rem(c, down_slots)]))
        return jnp.concatenate([high, low], axis=0)

    def project(c):
        side_acc[...] += dot_lanes(block[...], pout[:, chunk(c)])

    def refill(c):
        @pl.when(c + down_slots < steps)
        def _():
            down_copy(c + down_slots).start()

    block[...] = down_dot(0)
    refill(0)

    @pl.loop(1, steps)
    def _(c):
        new = down_dot(c)
        project(c - 1)
        block[...] = new
        refill(c)

    project(steps - 1)

    def sum_parts(parts):
        return lax.fori_loop(
            0, n, lambda p, t: t + parts[p], jnp.zeros(parts.shape[1:], F32), unroll=8
        )

    side = side_acc[:count, :] + side_acc[count:, :]
    own_row = lax.broadcasted_iota(jnp.int32, side.shape, 0) == me
    side = side - jnp.where(own_row, jnp.broadcast_to(target_side, side.shape), 0.0)
    payload_b[...] = pack(side)
    start_all(b_push)
    parts_b[me] = payload_b[...]
    marks = (
        lax.broadcasted_iota(jnp.int32, (2 * SEQS, count), 0) == segment_ids[...]
    ).astype(BF16)

    receive_all(a_push)
    total = sum_parts(parts_a)
    input_side = jnp.concatenate([total[:, :rank], total[:, rank:]], axis=0)
    high, low = split(input_side)
    wide = dot(jnp.concatenate([high, low], axis=0), expand[...])
    spread[...] = wide[:count] + wide[count:]
    loads[4].wait()

    receive_all(b_push)
    total = sum_parts(parts_b)
    first, second = total[:, :rank], total[:, rank:]
    doubled = jnp.concatenate(
        [jnp.concatenate([first, first], axis=1), jnp.concatenate([second, second], axis=1)],
        axis=0,
    )
    pairs = spread[...] * jnp.concatenate([doubled] * (rank // 2), axis=1)
    high, low = split(pairs)
    kronecker = dot(marks, high) + dot(marks, low)
    scores[...] = dot_lanes(kronecker.astype(BF16), qbuf[...])[:SEQS]

    @pl.loop(1, n)
    def _(d):
        token_push(d, me).wait_send()
        a_push(d, me).wait_send()
        b_push(d, me).wait_send()


def solution(mesh):
    n = mesh.shape["query"]

    def local(tokens, target, gate, up, down, proj_in, proj_out, segment_ids, queries):
        width, units = gate.shape
        rank = proj_in.shape[1]
        count = segment_ids.shape[0]
        pieces = width // LANES
        any_spec = pl.BlockSpec(memory_space=pl.ANY)
        vmem_spec = pl.BlockSpec(memory_space=pltpu.VMEM)
        dma = pltpu.SemaphoreType.DMA
        return pl.pallas_call(
            functools.partial(kernel, n),
            out_shape=jax.ShapeDtypeStruct((SEQS, queries.shape[0]), F32),
            in_specs=[any_spec] * 7 + [vmem_spec, any_spec],
            out_specs=vmem_spec,
            scratch_shapes=[
                pltpu.VMEM((SLOTS, DEPTH, units), BF16),
                pltpu.VMEM((SLOTS, DEPTH, units), BF16),
                pltpu.VMEM((DOWN_SLOTS, units, DEPTH), BF16),
                pltpu.VMEM((rank, units), BF16),
                pltpu.VMEM((rank, width), BF16),
                pltpu.VMEM((1, width), BF16),
                pltpu.VMEM((1, width), BF16),
                pltpu.VMEM(queries.shape, BF16),
                pltpu.VMEM((pieces, LANES), F32),
                pltpu.VMEM((pieces, LANES), BF16),
                pltpu.VMEM((n, pieces, LANES), BF16),
                pltpu.VMEM((n * pieces, LANES), F32),
                pltpu.VMEM((count, width), BF16),
                pltpu.VMEM((rank, rank * rank), BF16),
                pltpu.VMEM((count, rank * rank), F32),
                pltpu.VMEM((count, units), F32),
                pltpu.VMEM((count, units), F32),
                pltpu.VMEM((count, units), BF16),
                pltpu.VMEM((2 * count, DEPTH), BF16),
                pltpu.VMEM((2 * count, rank), F32),
                pltpu.VMEM((count // 2, 2 * rank), F32),
                pltpu.VMEM((count // 2, 2 * rank), F32),
                pltpu.VMEM((n, count // 2, 2 * rank), F32),
                pltpu.VMEM((n, count // 2, 2 * rank), F32),
                dma((SLOTS,)),
                dma((SLOTS,)),
                dma((DOWN_SLOTS,)),
                dma((5,)),
                dma((n,)),
                dma((n,)),
                dma((n,)),
                dma((n,)),
                dma((n,)),
                dma((n,)),
            ],
            compiler_params=pltpu.CompilerParams(
                collective_id=0, has_side_effects=True, vmem_limit_bytes=63 * 1024 * 1024
            ),
            name="forget",
        )(
            tokens, target, gate, up, down, proj_in.T, proj_out.T,
            segment_ids.reshape(1, count), queries,
        ).T

    in_specs = (
        P(("groups", "query"), None),
        P(("groups", "query"), None),
        P(None, "query"),
        P(None, "query"),
        P("query", None),
        P("query", None),
        P(),
        P("groups"),
        P("query", None),
    )
    return jax.shard_map(
        local, mesh=mesh, in_specs=in_specs, out_specs=P("query", "groups"), check_vma=False
    )
```

```python
import functools

import jax
import jax.numpy as jnp
from jax import lax
from jax.experimental import pallas as pl
from jax.experimental.pallas import tpu as pltpu
from jax.sharding import PartitionSpec as P

SEQS = 4
DEPTH = 1024
SLOTS = 5
DOWN_SLOTS = 4
LANES = 128
F32 = jnp.float32
BF16 = jnp.bfloat16
MESH = pl.DeviceIdType.MESH


def split(value):
    high = value.astype(BF16)
    return high, (value - high.astype(F32)).astype(BF16)


def dot(a, b):
    return jnp.dot(a, b, preferred_element_type=F32)


def dot_lanes(a, b):
    return lax.dot_general(a, b, (((1,), (1,)), ((), ())), preferred_element_type=F32)


def pack(value):
    half = value.shape[0] // 2
    return jnp.concatenate([value[:half], value[half:]], axis=1)


def kernel(
    n, tokens, target, gate, up, down, proj_in, proj_out, segment_ids, queries, scores,
    gate_ring, up_ring, down_ring, pin, pout, tok, tgt, qbuf, slab32, slab, gathered, x32, x16,
    expand, spread, gate_acc, up_acc, hidden_ref, block, side_acc, payload_a, payload_b, parts_a, parts_b,
    gate_sem, up_sem, down_sem, load_sem, tok_send, tok_recv, a_send, a_recv, b_send, b_recv,
):
    me = lax.axis_index("query")
    width = gate.shape[0]
    rank = proj_in.shape[0]
    count = x16.shape[0]
    pieces = width // LANES
    steps = width // DEPTH
    slots = gate_ring.shape[0]
    down_slots = down_ring.shape[0]

    def peer(d):
        return lax.rem(me + d, n)

    barrier = pltpu.get_barrier_semaphore()

    @pl.loop(1, n)
    def _(d):
        pl.semaphore_signal(barrier, inc=1, device_id={"query": peer(d)}, device_id_type=MESH)

    loads = [
        pltpu.make_async_copy(src, dst, load_sem.at[i])
        for i, (src, dst) in enumerate(
            [(tokens, tok), (target, tgt), (proj_out, pout), (proj_in, pin), (queries, qbuf)]
        )
    ]

    def chunk(c):
        return pl.ds(pl.multiple_of(c * DEPTH, DEPTH), DEPTH)

    def ring_copies(c, slot):
        return (
            pltpu.make_async_copy(gate.at[chunk(c), :], gate_ring.at[slot], gate_sem.at[slot]),
            pltpu.make_async_copy(up.at[chunk(c), :], up_ring.at[slot], up_sem.at[slot]),
        )

    def down_copy(c):
        slot = lax.rem(c, down_slots)
        return pltpu.make_async_copy(down.at[:, chunk(c)], down_ring.at[slot], down_sem.at[slot])

    for load in loads[:3]:
        load.start()
    for c in range(slots):
        for copy in ring_copies(c, c):
            copy.start()
    loads[3].start()
    loads[4].start()

    loads[0].wait()
    for k in range(pieces):
        slab32[k : k + 1, :] = tok[:, k * LANES : (k + 1) * LANES].astype(F32)
    slab[...] = slab32[...].astype(BF16)
    gathered[me] = slab[...]

    pl.semaphore_wait(barrier, n - 1)

    def push(src, dst, send, recv, d, slot):
        return pltpu.make_async_remote_copy(
            src_ref=src,
            dst_ref=dst.at[slot],
            send_sem=send.at[d],
            recv_sem=recv.at[slot],
            device_id={"query": peer(d)},
            device_id_type=MESH,
        )

    token_push = functools.partial(push, slab, gathered, tok_send, tok_recv)
    a_push = functools.partial(push, payload_a, parts_a, a_send, a_recv)
    b_push = functools.partial(push, payload_b, parts_b, b_send, b_recv)

    def start_all(copy):
        @pl.loop(1, n)
        def _(d):
            copy(d, me).start()

    def receive_all(copy):
        @pl.loop(1, n)
        def _(d):
            copy(d, peer(d)).wait_recv()

    start_all(token_push)

    owner = lax.broadcasted_iota(jnp.int32, expand.shape, 1) // rank
    expand[...] = jnp.where(
        lax.broadcasted_iota(jnp.int32, expand.shape, 0) == owner, 1.0, 0.0
    ).astype(BF16)
    gate_acc[...] = jnp.zeros_like(gate_acc)
    up_acc[...] = jnp.zeros_like(up_acc)
    side_acc[...] = jnp.zeros_like(side_acc)
    loads[1].wait()
    loads[2].wait()
    target_side = dot_lanes(tgt[...], pout[...])

    receive_all(token_push)
    x32[...] = gathered[...].reshape(n * pieces, LANES).astype(F32)
    for k in range(pieces):
        x16[:, k * LANES : (k + 1) * LANES] = x32[pl.ds(k, n, stride=pieces), :].astype(BF16)

    @pl.loop(0, steps)
    def _(c):
        slot = lax.rem(c, slots)
        for copy in ring_copies(c, slot):
            copy.wait()
        x = x16[:, chunk(c)]
        gate_acc[...] += dot(x, gate_ring[slot])
        up_acc[...] += dot(x, up_ring[slot])

        @pl.when(c + slots < steps)
        def _():
            for copy in ring_copies(c + slots, slot):
                copy.start()

        @pl.when(c < down_slots)
        def _():
            down_copy(c).start()

    gate_pre = gate_acc[...]
    hidden = (gate_pre / (1.0 + jnp.exp(-gate_pre)) * up_acc[...]).astype(BF16)
    hidden_ref[...] = hidden
    loads[3].wait()
    payload_a[...] = pack(dot_lanes(hidden, pin[...]))
    start_all(a_push)
    parts_a[me] = payload_a[...]

    def down_dot(c):
        down_copy(c).wait()
        high, low = split(dot(hidden_ref[...], down_ring[lax.rem(c, down_slots)]))
        return jnp.concatenate([high, low], axis=0)

    def project(c):
        side_acc[...] += dot_lanes(block[...], pout[:, chunk(c)])

    def refill(c):
        @pl.when(c + down_slots < steps)
        def _():
            down_copy(c + down_slots).start()

    block[...] = down_dot(0)
    refill(0)

    @pl.loop(1, steps)
    def _(c):
        new = down_dot(c)
        project(c - 1)
        block[...] = new
        refill(c)

    project(steps - 1)

    def sum_parts(parts):
        return lax.fori_loop(
            0, n, lambda p, t: t + parts[p], jnp.zeros(parts.shape[1:], F32), unroll=8
        )

    side = side_acc[:count, :] + side_acc[count:, :]
    own_row = lax.broadcasted_iota(jnp.int32, side.shape, 0) == me
    side = side - jnp.where(own_row, jnp.broadcast_to(target_side, side.shape), 0.0)
    payload_b[...] = pack(side)
    start_all(b_push)
    parts_b[me] = payload_b[...]
    segments = jnp.concatenate([segment_ids[...], segment_ids[...]], axis=1)
    marks = (
        lax.broadcasted_iota(jnp.int32, (2 * SEQS, 2 * count), 0) == segments
    ).astype(BF16)

    receive_all(a_push)
    total = sum_parts(parts_a)
    input_side = jnp.concatenate([total[:, :rank], total[:, rank:]], axis=0)
    high, low = split(input_side)
    wide = dot(jnp.concatenate([high, low], axis=0), expand[...])
    spread[...] = wide[:count] + wide[count:]
    loads[4].wait()

    @pl.loop(1, n)
    def _(d):
        token_push(d, me).wait_send()
        a_push(d, me).wait_send()
        b_push(d, me).wait_send()

    receive_all(b_push)
    total = sum_parts(parts_b)
    first, second = total[:, :rank], total[:, rank:]
    doubled = jnp.concatenate(
        [jnp.concatenate([first, first], axis=1), jnp.concatenate([second, second], axis=1)],
        axis=0,
    )
    pairs = spread[...] * jnp.concatenate([doubled] * (rank // 2), axis=1)
    high, low = split(pairs)
    kronecker = dot(marks, jnp.concatenate([high, low], axis=0))
    scores[...] = dot_lanes(kronecker.astype(BF16), qbuf[...])[:SEQS]


def solution(mesh):
    n = mesh.shape["query"]

    def local(tokens, target, gate, up, down, proj_in, proj_out, segment_ids, queries):
        width, units = gate.shape
        rank = proj_in.shape[1]
        count = segment_ids.shape[0]
        pieces = width // LANES
        any_spec = pl.BlockSpec(memory_space=pl.ANY)
        vmem_spec = pl.BlockSpec(memory_space=pltpu.VMEM)
        dma = pltpu.SemaphoreType.DMA
        return pl.pallas_call(
            functools.partial(kernel, n),
            out_shape=jax.ShapeDtypeStruct((SEQS, queries.shape[0]), F32),
            in_specs=[any_spec] * 7 + [vmem_spec, any_spec],
            out_specs=vmem_spec,
            scratch_shapes=[
                pltpu.VMEM((SLOTS, DEPTH, units), BF16),
                pltpu.VMEM((SLOTS, DEPTH, units), BF16),
                pltpu.VMEM((DOWN_SLOTS, units, DEPTH), BF16),
                pltpu.VMEM((rank, units), BF16),
                pltpu.VMEM((rank, width), BF16),
                pltpu.VMEM((1, width), BF16),
                pltpu.VMEM((1, width), BF16),
                pltpu.VMEM(queries.shape, BF16),
                pltpu.VMEM((pieces, LANES), F32),
                pltpu.VMEM((pieces, LANES), BF16),
                pltpu.VMEM((n, pieces, LANES), BF16),
                pltpu.VMEM((n * pieces, LANES), F32),
                pltpu.VMEM((count, width), BF16),
                pltpu.VMEM((rank, rank * rank), BF16),
                pltpu.VMEM((count, rank * rank), F32),
                pltpu.VMEM((count, units), F32),
                pltpu.VMEM((count, units), F32),
                pltpu.VMEM((count, units), BF16),
                pltpu.VMEM((2 * count, DEPTH), BF16),
                pltpu.VMEM((2 * count, rank), F32),
                pltpu.VMEM((count // 2, 2 * rank), F32),
                pltpu.VMEM((count // 2, 2 * rank), F32),
                pltpu.VMEM((n, count // 2, 2 * rank), F32),
                pltpu.VMEM((n, count // 2, 2 * rank), F32),
                dma((SLOTS,)),
                dma((SLOTS,)),
                dma((DOWN_SLOTS,)),
                dma((5,)),
                dma((n,)),
                dma((n,)),
                dma((n,)),
                dma((n,)),
                dma((n,)),
                dma((n,)),
            ],
            compiler_params=pltpu.CompilerParams(
                collective_id=0, has_side_effects=True, vmem_limit_bytes=63 * 1024 * 1024
            ),
            name="forget",
        )(
            tokens, target, gate, up, down, proj_in.T, proj_out.T,
            segment_ids.reshape(1, count), queries,
        ).T

    in_specs = (
        P(("groups", "query"), None),
        P(("groups", "query"), None),
        P(None, "query"),
        P(None, "query"),
        P("query", None),
        P("query", None),
        P(),
        P("groups"),
        P("query", None),
    )
    return jax.shard_map(
        local, mesh=mesh, in_specs=in_specs, out_specs=P("query", "groups"), check_vma=False
    )
```
